128 devices in a mesh: space: 32 (over y_lo, z, x), vel: 4 (over y_hi, core).
Axes of the slice: x: 4, y: 4 (y_hi: 2, y_lo: 2; y = y_hi * 2 + y_lo), z: 4, core: 2. Of those that a mesh axis runs over, the one named last changes fastest.
Arguments:
- probe_field: float32 [2, 1024, 1024], P(None, 'space'), may hold values from -6 to 6
- control_field: float32 [2, 1024, 1024], P(None, 'space'), may hold values from -4 to 4
- optical_state: float32 [2, 64, 1024, 1024], P(None, 'vel', 'space'), may hold values from -3 to 3
- spin_state: float32 [2, 64, 1024, 1024], P(None, 'vel', 'space'), may hold values from -3 to 3
- doppler_shift: float32 [64], P('vel'), may hold values from -3 to 3
- class_weight: float32 [64], P('vel'), may hold values from 0.2 to 2
- gradient_shift: float32 [1024, 1024], P('space'), may hold values from -3 to 3
Outputs:
- probe_out: float32 [2, 1024, 1024], P(None, 'space')
- control_out: float32 [2, 1024, 1024], P(None, 'space')
- optical_out: float32 [2, 64, 1024, 1024], P(None, 'vel', 'space')
- spin_out: float32 [2, 64, 1024, 1024], P(None, 'vel', 'space')
The draws below stay inside these ranges and needn't reach their ends.
All inputs are finite; a program needn't handle non-finite values.
Results may differ from the reference program's by a relative error of at most 0.000098.
Values sent between devices are 32-bit elements; how exact they have to be, the bound alone decides.
No kernel may reach another device: no remote copies, remote signals or barrier semaphores. Data moves between devices by JAX's collectives and lax.ppermute only.
A program may use at most 128 MiB of HBM per device.

```python
import math
import jax
import jax.numpy as jnp
from jax import lax

GRID = 1024
VEL = 64


def block_levels(key, dims, shards, least, high):
    loudness = 1.0
    for position, shards_of in shards:
        draws = jax.random.uniform(jax.random.fold_in(jax.random.fold_in(key, 6), position), (shards_of,), jnp.float32, least / len(shards), high / len(shards))
        loudness = loudness * jnp.repeat(jnp.exp(draws), dims[position] // shards_of).reshape((-1,) + (1,) * (len(dims) - 1 - position))
    return loudness


def scatter_about(key, extent, spread, reach, cuts=(), kind=jnp.bfloat16):
    level = block_levels(key, extent, cuts, -0.22, 0.18) if cuts else 1.0
    values = jax.random.normal(key, extent, jnp.float32) * spread * level
    return jnp.minimum(jnp.maximum(values, -reach), reach).astype(kind)


def setup_inputs(seed: int = 0) -> dict:
    seeds = jax.random.split(jax.random.key(seed), 8)
    return {
        "probe_field": scatter_about(seeds[0], (2, GRID, GRID), 1.0, 6.0, ((1, 32),), jnp.float32),
        "control_field": scatter_about(seeds[1], (2, GRID, GRID), 1.0, 4.0, ((1, 32),), jnp.float32),
        "optical_state": scatter_about(seeds[2], (2, VEL, GRID, GRID), 0.5, 3.0, ((1, 4), (2, 32)), jnp.float32),
        "spin_state": scatter_about(seeds[3], (2, VEL, GRID, GRID), 0.5, 3.0, ((1, 4), (2, 32)), jnp.float32),
        "doppler_shift": scatter_about(seeds[4], (VEL,), 1.0, 3.0, ((0, 4),), jnp.float32),
        "class_weight": jnp.clip(jnp.exp(math.log(2.0) - 2.3025851 * jax.random.uniform(seeds[5], (VEL,), jnp.float32) ** block_levels(seeds[5], (VEL,), ((0, 4),), -0.2, 0.2)), 0.2, 2.0),
        "gradient_shift": scatter_about(seeds[6], (GRID, GRID), 1.0, 3.0, ((0, 32),), jnp.float32),
    }


GAMMA = 1.0
DEPHASE = 0.1
DT = 0.25
COUPLE = 2.0


def phase_angles(grid_width):
    counter = jnp.arange(grid_width, dtype=jnp.int32)
    frequency = jnp.where(counter < grid_width // 2, counter, counter - grid_width)
    return jnp.pi * ((frequency * frequency) % (2 * grid_width)).astype(jnp.float32) / grid_width


def diffract(complex_field, phase_plane):
    wavefront = complex_field[0] + 1j * complex_field[1]
    result = jnp.fft.ifft2(jnp.fft.fft2(wavefront) * phase_plane)
    return jnp.stack([jnp.real(result), jnp.imag(result)]).astype(jnp.float32)


def derivative(optical, spin_part, probe_part, control, doppler, gradient):
    optical_real, optical_imag = optical[0], optical[1]
    spin_real, spin_imag = spin_part[0], spin_part[1]
    probe_real, probe_imag = probe_part[0], probe_part[1]
    control_real, control_imag = control[0], control[1]
    rate_optical_real = -GAMMA * optical_real + doppler * optical_imag - probe_imag - (control_real * spin_imag + control_imag * spin_real)
    rate_optical_imag = -GAMMA * optical_imag - doppler * optical_real + probe_real + (control_real * spin_real - control_imag * spin_imag)
    rate_spin_real = -DEPHASE * spin_real + gradient * spin_imag - (control_real * optical_imag - control_imag * optical_real)
    rate_spin_imag = -DEPHASE * spin_imag - gradient * spin_real + (control_real * optical_real + control_imag * optical_imag)
    return jnp.stack([rate_optical_real, rate_optical_imag]), jnp.stack([rate_spin_real, rate_spin_imag])


def midpoint(optical, spin_part, probe_part, control, doppler, gradient):
    rate_optical, rate_spin = derivative(optical, spin_part, probe_part, control, doppler, gradient)
    half_optical = optical + 0.5 * DT * rate_optical
    half_spin = spin_part + 0.5 * DT * rate_spin
    rate_optical, rate_spin = derivative(half_optical, half_spin, probe_part, control, doppler, gradient)
    return optical + DT * rate_optical, spin_part + DT * rate_spin


def reference(probe_field, control_field, optical_state, spin_state, doppler_shift, class_weight, gradient_shift):
    angles = phase_angles(GRID)
    phase_plane = jnp.exp(-1j * (angles[:, None] + angles[None, :]))
    probe_one = diffract(probe_field, phase_plane)
    control_one = diffract(control_field, phase_plane)
    optical_classes = jnp.moveaxis(optical_state, 1, 0)
    spin_classes = jnp.moveaxis(spin_state, 1, 0)

    def advance(class_item):
        optical, spin_part, doppler = class_item
        return midpoint(optical, spin_part, probe_one, control_one, doppler, gradient_shift)

    optical_new, spin_new = lax.map(advance, (optical_classes, spin_classes, doppler_shift))
    polarization = jnp.einsum('vcrn,v->crn', optical_new, class_weight, precision=lax.Precision.HIGHEST) / VEL
    probe_two = jnp.stack([probe_one[0] - COUPLE * polarization[1], probe_one[1] + COUPLE * polarization[0]])
    probe_out = diffract(probe_two, phase_plane)
    control_out = diffract(control_one, phase_plane)
    return probe_out, control_out, jnp.moveaxis(optical_new, 0, 1), jnp.moveaxis(spin_new, 0, 1)
```

```python
import jax
import jax.numpy as jnp
import numpy as np
from jax import lax
from jax.experimental import pallas as pl
from jax.experimental.pallas import tpu as pltpu
from jax.sharding import Mesh
from jax.sharding import PartitionSpec as P


N = 1024
BF16 = jnp.bfloat16
F32 = jnp.float32


def turn(numerator, period):
    angle = 2.0 * np.pi * (np.asarray(numerator, np.int64) % period) / period
    return np.cos(angle) + 1j * np.sin(angle)


NORM = np.exp(-0.25j * np.pi) / 32.0


def chirp(n):
    return turn(np.asarray(n, np.int64) ** 2, 2 * N)


def pair(z):
    return np.stack([z.real, z.imag]).astype(np.float32)


def halves(x):
    x = np.asarray(x, np.float32)
    high = x.astype(BF16)
    low = (x - high.astype(np.float32)).astype(BF16)
    return np.stack([high, low])


def row_tables():
    n = np.arange(N)
    pre = pair(NORM * chirp(n))
    short = np.arange(256)
    twiddle = pair(turn(-np.arange(4)[:, None] * short[None, :], N)).reshape(8, 256)
    dft = turn(-np.arange(128)[:, None] * short[None, :], 256)
    table = halves(np.concatenate([dft.real, dft.imag], axis=0))
    out = 4 * np.arange(128)[:, None] + np.repeat(np.arange(4), 32)[None, :]
    return pre, twiddle, table, pair(chirp(out))


def column_tables():
    eye = np.eye(4)
    small = turn(-np.arange(32)[:, None] * np.arange(32)[None, :], 32)
    right = np.concatenate([np.kron(eye, small.real), np.kron(eye, small.imag)], axis=1)
    inner = np.tile(np.arange(32), 4)
    twiddle = pair(turn(-inner[:, None] * inner[None, :], N))
    wave = chirp(32 * inner[:, None] + inner[None, :])
    return halves(right), halves(right.T), twiddle, pair(wave), pair(NORM * wave)


def last_tables():
    c2, h, c1, t = np.meshgrid(np.arange(2), np.arange(2), np.arange(4), np.arange(16), indexing="ij")
    quarter = (128 * h + 16 * (2 * c1 + c2) + t).reshape(-1)
    classes = np.arange(4)
    pre = pair(NORM * chirp(4 * quarter[None, :] + classes[:, None])).reshape(8, 256)
    short = np.arange(256)
    dft = turn(-quarter[:, None] * short[None, :], 256)
    table = halves(np.concatenate([dft.real, dft.imag], axis=1))
    twiddle = pair(turn(-classes[:, None] * short[None, :], N)).reshape(8, 256)
    return pre, table, twiddle, pair(chirp(np.arange(N)))


def split(x):
    high = x.astype(BF16)
    return high, (x - high.astype(F32)).astype(BF16)


def mm(a, b, dims):
    return lax.dot_general(a, b, (dims, ((), ())), preferred_element_type=F32)


def mm3(a, b, dims):
    (ah, al), (bh, bl) = a, b
    return mm(ah, bh, dims) + (mm(ah, bl, dims) + mm(al, bh, dims))


def cmul(xr, xi, yr, yi):
    return xr * yr - xi * yi, xr * yi + xi * yr


def butterfly(r, i):
    ar, ai, br, bi = r[0] + r[2], i[0] + i[2], r[0] - r[2], i[0] - i[2]
    cr, ci, dr, di = r[1] + r[3], i[1] + i[3], r[1] - r[3], i[1] - i[3]
    return (
        [ar + cr, br + di, ar - cr, br - di],
        [ai + ci, bi - dr, ai - ci, bi + dr],
    )


def rows_kernel(probe, control, pre, twiddle, table, post, out):
    core, half = lax.axis_index("co"), lax.axis_index("yh")
    first = half == 0
    xr = jnp.where(first, probe[0], control[0])
    xi = jnp.where(first, probe[1], control[1])
    lane = lax.broadcasted_iota(jnp.int32, (1, N), 1)
    sign = jnp.where((lane & core) == 1, -1.0, 1.0)
    xr, xi = cmul(xr, xi, pre[0:1, :] * sign, pre[1:2, :] * sign)
    r, i = butterfly(
        [xr[:, 256 * k : 256 * k + 256] for k in range(4)],
        [xi[:, 256 * k : 256 * k + 256] for k in range(4)],
    )
    for p in range(1, 4):
        r[p], i[p] = cmul(r[p], i[p], twiddle[p : p + 1, :], twiddle[4 + p : 5 + p, :])
    x = split(jnp.concatenate(r + i, axis=0))
    o = mm3((table[0], table[1]), x, ((1,), (1,)))
    yr = o[:128, :128] - o[128:, 128:]
    yi = o[:128, 128:] + o[128:, :128]
    lane = lax.broadcasted_iota(jnp.int32, (1, 128), 1)
    sign = jnp.where(((lane // 32) & core) == 1, -1.0, 1.0)
    yr, yi = cmul(yr, yi, post[0] * sign, post[1] * sign)
    for c1 in range(4):
        for p in range(4):
            piece = [
                y[16 * (2 * c1 + c2) : 16 * (2 * c1 + c2) + 16, 32 * p : 32 * p + 32]
                for y in (yr, yi)
                for c2 in range(2)
            ]
            out[pl.ds(4 * p + c1, 16, stride=16), :] = jnp.concatenate(piece, axis=1)


def sums_kernel(doppler, weight, a, b, gradient, own, other):
    core = lax.axis_index("co")
    for out, half in ((own, core), (other, 1 - core)):

        def tile(j, _, out=out, half=half):
            cols = pl.ds(pl.multiple_of(half * 512 + 128 * j, 128), 128)
            here = pl.ds(pl.multiple_of(128 * j, 128), 128)
            acc = None
            for v in range(16):
                d, w = doppler[v], weight[v]
                wd = w * d
                w1 = w * (0.78125 - 0.03125 * d * d)
                ar, ai = a[0, v, :, cols], a[1, v, :, cols]
                br, bi = b[0, v, :, cols], b[1, v, :, cols]
                new = (
                    w1 * ar, w1 * ai, wd * ar, wd * ai, w * ar, w * ai,
                    w * br, w * bi, wd * br, wd * bi,
                )
                acc = new if acc is None else tuple(x + y for x, y in zip(acc, new))
            r1r, r1i, r2r, r2i, s2r, s2i, s4r, s4i, t4r, t4i = acc
            g = 0.03125 * gradient[:, cols]
            out[0, :, here] = r1r + 0.1875 * r2i
            out[1, :, here] = r1i - 0.1875 * r2r
            out[2, :, here] = s2r
            out[3, :, here] = s2i
            out[4, :, here] = 0.215625 * s4r + 0.03125 * t4i + g * s4i
            out[5, :, here] = 0.215625 * s4i - 0.03125 * t4r - g * s4r
            return 0

        lax.fori_loop(0, 4, tile, 0)


def pack_kernel(own, other, fields, out):
    for k in range(6):
        s = own[k] + other[k]
        s = jnp.concatenate([s[:, 128 * c : 128 * c + 128] for c in range(4)], axis=0).T
        for c2 in range(2):
            out[pl.ds(2 * k + c2, 64, stride=16), :] = s[64 * c2 : 64 * c2 + 64]
    for c1 in range(4):
        out[pl.ds(12 + c1, 64, stride=16), :] = fields[pl.ds(c1, 64, stride=4), :]


def columns_kernel(d0, d1, d2, d3, got, right, left, twiddle, wave, pre, out):
    def transform(xr, xi):
        yr, yi = cmul(xr, xi, pre[0], pre[1])
        y = split(jnp.concatenate([yr.T, yi.T], axis=0))
        o = mm3(y, (right[0], right[1]), ((1,), (0,)))
        ur = o[:128, :128] - o[128:, 128:]
        ui = o[:128, 128:] + o[128:, :128]
        vr, vi = cmul(ur, ui, twiddle[0], twiddle[1])
        v = split(jnp.concatenate([vr, vi], axis=1))
        o = mm3((left[0], left[1]), v, ((1,), (0,)))
        wr = o[:128, :128] - o[128:, 128:]
        wi = o[:128, 128:] + o[128:, :128]
        return cmul(wr, wi, wave[0], wave[1])

    x0, x1 = (
        jnp.concatenate([got[pl.ds(16 * f + 12 + c1, 32, stride=32), :] for c1 in range(4)], axis=0)
        for f in range(2)
    )
    low = lax.broadcasted_iota(jnp.int32, (128, 128), 1) < 64
    xr = jnp.where(low, x0, pltpu.roll(x1, 64, 1))
    xi = jnp.where(low, pltpu.roll(x0, 64, 1), x1)
    zr, zi = transform(xr, xi)
    for y in range(2):
        for f in range(2):
            for c2 in range(2):
                at = slice(64 * f + 32 * c2, 64 * f + 32 * c2 + 32)
                out[pl.ds(16 * y + 4 * f + c2, 32, stride=32), :] = zr[at]
                out[pl.ds(16 * y + 4 * f + 2 + c2, 32, stride=32), :] = zi[at]

    gr = jnp.float32(0.0)
    gi = jnp.float32(0.0)
    for d in (d0, d1, d2, d3):
        for v in range(16):
            gr = gr + d[0, v]
            gi = gi + d[0, v] * d[1, v]
    gr, gi = 0.21875 * gr, -0.03125 * gi

    def total(k):
        return jnp.concatenate(
            [
                got[pl.ds(2 * k + c2, 32, stride=32), :] + got[pl.ds(16 + 2 * k + c2, 32, stride=32), :]
                for c2 in range(2)
            ],
            axis=0,
        )

    s1r, s1i, s2r, s2i, s3r, s3i = (total(k) for k in range(6))
    er, ei, cr, ci = zr[:64], zi[:64], zr[64:], zi[64:]
    q = 0.03125 * (cr * cr + ci * ci)
    tr = s1r - q * s2r - (cr * s3i + ci * s3r) - (er * gi + ei * gr)
    ti = s1i - q * s2i + (cr * s3r - ci * s3i) + (er * gr - ei * gi)
    pr = er - 0.03125 * ti
    pi = ei + 0.03125 * tr
    zr, zi = transform(jnp.concatenate([pr, cr], axis=0), jnp.concatenate([pi, ci], axis=0))
    for y in range(2):
        for c1 in range(4):
            at = slice(32 * c1, 32 * c1 + 32)
            out[pl.ds(16 * y + 8 + c1, 32, stride=32), :] = zr[at]
            out[pl.ds(16 * y + 12 + c1, 32, stride=32), :] = zi[at]


def step_kernel(doppler, own, other, a, b, gradient, a_out, b_out, fields):
    core = lax.axis_index("co")

    @pl.when(pl.program_id(0) == 0)
    def _():
        for got, half in ((own, core), (other, 1 - core)):
            for k in range(4):
                x = jnp.concatenate([got[pl.ds(2 * k + c2, 64, stride=16), :] for c2 in range(2)], axis=0).T
                for c1 in range(4):
                    cols = pl.ds(pl.multiple_of(half * 512 + 128 * c1, 128), 128)
                    fields[k, :, cols] = x[32 * c1 : 32 * c1 + 32]

    rows = pl.ds(pl.multiple_of(8 * pl.program_id(0), 8), 8)

    def tile(j, _):
        cols = pl.ds(pl.multiple_of(128 * j, 128), 128)
        er, ei, cr, ci = (fields[k, rows, cols] for k in range(4))
        d = gradient[:, cols]
        d3 = 0.03125 * d
        q = 0.03125 * (cr * cr + ci * ci)
        wr, wi = d3 * cr - 0.215625 * ci, 0.215625 * cr + d3 * ci
        vr, vi = d3 * cr + 0.215625 * ci, 0.215625 * cr - d3 * ci
        lr = 0.9753125 - d3 * d - q
        li = -0.24375 * d
        yr = -0.03125 * (cr * er + ci * ei)
        yi = -0.03125 * (cr * ei - ci * er)
        fr, fi = -0.21875 * ei, 0.21875 * er
        for v in range(16):
            dv = doppler[v]
            dv3 = 0.03125 * dv
            kr = 0.78125 - dv3 * dv
            ki = -0.1875 * dv
            ar, ai = a[0, v, :, cols], a[1, v, :, cols]
            br, bi = b[0, v, :, cols], b[1, v, :, cols]
            mr = kr - q
            gr, gi = dv3 * cr, dv3 * ci
            ur, ui = wr + gr, wi + gi
            tr, ti = vr + gr, vi - gi
            a_out[0, v, :, cols] = (mr * ar - ki * ai) + (ur * br - ui * bi) + (fr + dv3 * er)
            a_out[1, v, :, cols] = (mr * ai + ki * ar) + (ur * bi + ui * br) + (fi + dv3 * ei)
            b_out[0, v, :, cols] = (lr * br - li * bi) + (tr * ar - ti * ai) + yr
            b_out[1, v, :, cols] = (lr * bi + li * br) + (tr * ai + ti * ar) + yi
        return 0

    lax.fori_loop(0, 8, tile, 0)


def last_kernel(own, other, pre, table, twiddle, post, probe_out, control_out):
    zero = lax.axis_index("co") == 0
    x = []
    for k in range(4):
        parts = []
        for comp in range(2):
            pieces = []
            for h in range(2):
                for c1 in range(4):
                    at = pl.ds(16 * k + 8 + 4 * comp + c1, 16, stride=64)
                    mine, theirs = own[at, :], other[at, :]
                    pieces.append(jnp.where(zero, *((mine, theirs) if h == 0 else (theirs, mine))))
            z = jnp.concatenate(pieces, axis=0).T
            z = [jnp.concatenate([z[64 * f : 64 * f + 32], z[64 * f + 32 : 64 * f + 64]], axis=1) for f in range(2)]
            parts.append(jnp.concatenate(z, axis=0))
        x.extend(cmul(*parts, pre[k : k + 1, :], pre[4 + k : 5 + k, :]))
    o = mm3(split(jnp.concatenate(x, axis=0)), (table[0], table[1]), ((1,), (0,)))
    r, i = [], []
    for k in range(4):
        top, low = o[128 * k : 128 * k + 64], o[128 * k + 64 : 128 * k + 128]
        yr = top[:, :256] - low[:, 256:]
        yi = top[:, 256:] + low[:, :256]
        if k:
            yr, yi = cmul(yr, yi, twiddle[k : k + 1, :], twiddle[4 + k : 5 + k, :])
        r.append(yr)
        i.append(yi)
    r, i = butterfly(r, i)
    for k in range(4):
        at = slice(256 * k, 256 * k + 256)
        yr, yi = cmul(r[k], i[k], post[0:1, at], post[1:2, at])
        probe_out[0, :, at], probe_out[1, :, at] = yr[:32], yi[:32]
        control_out[0, :, at], control_out[1, :, at] = yr[32:], yi[32:]


SMEM = pl.BlockSpec(memory_space=pltpu.SMEM)
VMEM = pl.BlockSpec(memory_space=pltpu.VMEM)


def whole(kernel, count, shapes, scalars=0, **kwargs):
    return pl.pallas_call(
        kernel,
        out_shape=shapes,
        in_specs=[SMEM] * scalars + [VMEM] * count,
        out_specs=jax.tree.map(lambda _: VMEM, shapes),
        **kwargs,
    )


def f32(*shape):
    return jax.ShapeDtypeStruct(shape, F32)


STATE = pl.BlockSpec((2, 16, 8, N), lambda i: (0, 0, i, 0))
SHIFT = pl.BlockSpec((8, N), lambda i: (i, 0))


def shards(probe, control, optical, spin, doppler, weight, gradient):
    swap = [(0, 1), (1, 0)]
    both = [(k, 3 - k) for k in range(4)]
    mine = jnp.stack([weight, doppler])
    shifts = (
        mine,
        lax.ppermute(mine, "co", swap),
        lax.ppermute(mine, "yh", swap),
        lax.ppermute(mine, ("yh", "co"), both),
    )
    sums = pl.BlockSpec((6, 8, 512), lambda i: (0, i, 0))
    own, other = pl.pallas_call(
        sums_kernel,
        grid=(4,),
        out_shape=(f32(6, 32, 512), f32(6, 32, 512)),
        in_specs=[SMEM, SMEM, STATE, STATE, SHIFT],
        out_specs=(sums, sums),
        name="sums",
    )(doppler, weight, optical, spin, gradient)
    other = lax.ppermute(other, "co", swap)
    tables = [jnp.asarray(t) for t in row_tables()]
    fields = whole(rows_kernel, 6, f32(256, 128), name="rows")(probe, control, *tables)
    message = whole(pack_kernel, 3, f32(N, 128), name="pack")(own, other, fields)

    def exchange(x):
        x = lax.all_to_all(x.reshape(64, 16, 128), ("space", "yh"), 0, 0, tiled=True)
        return x.reshape(N, 128)

    tables = [jnp.asarray(t) for t in column_tables()]
    message = whole(columns_kernel, 6, f32(N, 128), 4, name="columns")(
        *shifts, exchange(message), *tables
    )
    got = exchange(message)
    other = lax.ppermute(got, "co", swap)
    optical_out, spin_out = pl.pallas_call(
        step_kernel,
        grid=(4,),
        out_shape=(f32(*optical.shape), f32(*spin.shape)),
        in_specs=[SMEM, VMEM, VMEM, STATE, STATE, SHIFT],
        out_specs=(STATE, STATE),
        scratch_shapes=[pltpu.VMEM((4, 32, N), F32)],
        name="step",
    )(doppler, got, other, optical, spin, gradient)
    tables = [jnp.asarray(t) for t in last_tables()]
    probe_out, control_out = whole(last_kernel, 6, (f32(2, 32, N), f32(2, 32, N)), name="last")(
        got, other, *tables
    )
    return probe_out, control_out, optical_out, spin_out


def solution(mesh):
    fine = Mesh(mesh.devices.reshape(mesh.devices.shape[0], 2, 2), ("space", "yh", "co"))
    vel = ("yh", "co")
    field, state = P(None, "space", None), P(None, vel, "space", None)
    return jax.shard_map(
        shards,
        mesh=fine,
        in_specs=(field, field, state, state, P(vel), P(vel), P("space", None)),
        out_specs=(field, field, state, state),
        check_vma=False,
    )
```

```python
import jax
import jax.numpy as jnp
import numpy as np
from jax import lax
from jax.experimental import pallas as pl
from jax.experimental.pallas import tpu as pltpu
from jax.sharding import Mesh
from jax.sharding import PartitionSpec as P


N = 1024
BF16 = jnp.bfloat16
F32 = jnp.float32


def turn(numerator, period):
    angle = 2.0 * np.pi * (np.asarray(numerator, np.int64) % period) / period
    return np.cos(angle) + 1j * np.sin(angle)


NORM = np.exp(-0.25j * np.pi) / 32.0


def chirp(n):
    return turn(np.asarray(n, np.int64) ** 2, 2 * N)


def pair(z):
    return np.stack([z.real, z.imag]).astype(np.float32)


def halves(x):
    x = np.asarray(x, np.float32)
    high = x.astype(BF16)
    low = (x - high.astype(np.float32)).astype(BF16)
    return np.stack([high, low])


def row_tables():
    n = np.arange(N)
    pre = pair(NORM * chirp(n))
    short = np.arange(256)
    twiddle = pair(turn(-np.arange(4)[:, None] * short[None, :], N)).reshape(8, 256)
    dft = turn(-np.arange(128)[:, None] * short[None, :], 256)
    table = halves(np.concatenate([dft.real, dft.imag], axis=0))
    out = 4 * np.arange(128)[:, None] + np.repeat(np.arange(4), 32)[None, :]
    return pre, twiddle, table, pair(chirp(out))


def column_tables():
    eye = np.eye(4)
    small = turn(-np.arange(32)[:, None] * np.arange(32)[None, :], 32)
    right = np.concatenate([np.kron(eye, small.real), np.kron(eye, small.imag)], axis=1)
    inner = np.tile(np.arange(32), 4)
    twiddle = pair(turn(-inner[:, None] * inner[None, :], N))
    wave = chirp(32 * inner[:, None] + inner[None, :])
    return halves(right), halves(right.T), twiddle, pair(wave), pair(NORM * wave)


def last_tables():
    c2, h, c1, t = np.meshgrid(np.arange(2), np.arange(2), np.arange(4), np.arange(16), indexing="ij")
    quarter = (128 * h + 16 * (2 * c1 + c2) + t).reshape(-1)
    classes = np.arange(4)
    pre = pair(NORM * chirp(4 * quarter[None, :] + classes[:, None])).reshape(8, 256)
    short = np.arange(256)
    dft = turn(-quarter[:, None] * short[None, :], 256)
    table = halves(np.concatenate([dft.real, dft.imag], axis=1))
    twiddle = pair(turn(-classes[:, None] * short[None, :], N)).reshape(8, 256)
    return pre, table, twiddle, pair(chirp(np.arange(N)))


def split(x):
    high = x.astype(BF16)
    return high, (x - high.astype(F32)).astype(BF16)


def mm(a, b, dims):
    return lax.dot_general(a, b, (dims, ((), ())), preferred_element_type=F32)


def mm3(a, b, dims):
    (ah, al), (bh, bl) = a, b
    return mm(ah, bh, dims) + (mm(ah, bl, dims) + mm(al, bh, dims))


def cmul(xr, xi, yr, yi):
    return xr * yr - xi * yi, xr * yi + xi * yr


def butterfly(r, i):
    ar, ai, br, bi = r[0] + r[2], i[0] + i[2], r[0] - r[2], i[0] - i[2]
    cr, ci, dr, di = r[1] + r[3], i[1] + i[3], r[1] - r[3], i[1] - i[3]
    return (
        [ar + cr, br + di, ar - cr, br - di],
        [ai + ci, bi - dr, ai - ci, bi + dr],
    )


def rows_part(x, core, pre, twiddle, table, post, out):
    lane = lax.broadcasted_iota(jnp.int32, (1, N), 1)
    sign = jnp.where((lane & core) == 1, -1.0, 1.0)
    xr, xi = cmul(x[0], x[1], pre[0:1, :] * sign, pre[1:2, :] * sign)
    r, i = butterfly(
        [xr[:, 256 * k : 256 * k + 256] for k in range(4)],
        [xi[:, 256 * k : 256 * k + 256] for k in range(4)],
    )
    for p in range(1, 4):
        r[p], i[p] = cmul(r[p], i[p], twiddle[p : p + 1, :], twiddle[4 + p : 5 + p, :])
    x = split(jnp.concatenate(r + i, axis=0))
    o = mm3((table[0], table[1]), x, ((1,), (1,)))
    yr = o[:128, :128] - o[128:, 128:]
    yi = o[:128, 128:] + o[128:, :128]
    lane = lax.broadcasted_iota(jnp.int32, (1, 128), 1)
    sign = jnp.where(((lane // 32) & core) == 1, -1.0, 1.0)
    yr, yi = cmul(yr, yi, post[0] * sign, post[1] * sign)
    for c1 in range(4):
        for p in range(4):
            piece = [
                y[16 * (2 * c1 + c2) : 16 * (2 * c1 + c2) + 16, 32 * p : 32 * p + 32]
                for y in (yr, yi)
                for c2 in range(2)
            ]
            out[pl.ds(4 * p + c1, 16, stride=16), :] = jnp.concatenate(piece, axis=1)


def front_kernel(
    doppler_hbm, weight_hbm, a_hbm, b_hbm, probe, control, gradient_hbm, pre_hbm, twiddle_hbm, table_hbm, post_hbm,
    own, other, fields, a, b, gradient, rates, x, pre, twiddle, table, post, doppler, weight, state_sem, sem,
):
    core, half = lax.axis_index("co"), lax.axis_index("yh")
    small = [
        pltpu.make_async_copy(src, dst, sem.at[k])
        for k, (src, dst) in enumerate(
            (
                (pre_hbm, pre),
                (twiddle_hbm, twiddle),
                (table_hbm, table),
                (post_hbm, post),
                (gradient_hbm, gradient),
                (doppler_hbm, doppler),
                (weight_hbm, weight),
            )
        )
    ]

    @pl.when(half == 0)
    def _():
        pltpu.make_async_copy(probe, x, sem.at[7]).start()

    @pl.when(half == 1)
    def _():
        pltpu.make_async_copy(control, x, sem.at[7]).start()

    for copy in small:
        copy.start()

    def chunk(n):
        rows = pl.ds(8 * (n // 2), 8)
        cols = pl.ds(pl.multiple_of((core if n % 2 else 1 - core) * 512, 512), 512)
        return [
            pltpu.make_async_copy(src.at[:, :, rows, cols], dst.at[:, :, rows, cols], state_sem.at[m, n])
            for m, (src, dst) in enumerate(((a_hbm, a), (b_hbm, b)))
        ]

    def start(n):
        for copy in chunk(n):
            copy.start()

    ahead = 4
    for n in range(ahead):
        start(n)

    pltpu.make_async_copy(probe, x, sem.at[7]).wait()
    for copy in small:
        copy.wait()
    rows_part(x, core, pre, twiddle, table, post, fields)
    gr, gi = 0.0, 0.0
    for v in range(16):
        gr = gr + weight[v]
        gi = gi + weight[v] * doppler[v]
    first = lax.broadcasted_iota(jnp.int32, (8, 512), 0) == 0
    for out in (own, other):
        out[192:200, :] = jnp.where(first, 0.21875 * gr, -0.03125 * gi)
    for v in range(16):
        d = doppler[v]
        for m, c in enumerate((0.03125 * d, 0.78125 - 0.03125 * d * d, -0.1875 * d)):
            rates[3 * v + m] = jnp.full((8, 128), c, F32)

    for n in range(8):
        for copy in chunk(n):
            copy.wait()
        if n + ahead < 8:
            start(n + ahead)
        k = n // 2
        rows = pl.ds(8 * k, 8)
        out, part = (own, core) if n % 2 else (other, 1 - core)

        def tile(j, _, out=out, part=part, rows=rows, k=k):
            cols = pl.ds(pl.multiple_of(part * 512 + 128 * j, 128), 128)
            here = pl.ds(pl.multiple_of(128 * j, 128), 128)
            acc = None
            for v in range(16):
                d, w = doppler[v], weight[v]
                wd = w * d
                w1 = w * (0.78125 - 0.03125 * d * d)
                ar, ai = a[0, v, rows, cols], a[1, v, rows, cols]
                br, bi = b[0, v, rows, cols], b[1, v, rows, cols]
                new = (
                    w1 * ar, w1 * ai, wd * ar, wd * ai, w * ar, w * ai,
                    w * br, w * bi, wd * br, wd * bi,
                )
                acc = new if acc is None else tuple(x + y for x, y in zip(acc, new))
            r1r, r1i, r2r, r2i, s2r, s2i, s4r, s4i, t4r, t4i = acc
            g = 0.03125 * gradient[rows, cols]
            s3r = 0.215625 * s4r + 0.03125 * t4i + g * s4i
            s3i = 0.215625 * s4i - 0.03125 * t4r - g * s4r
            s1r, s1i = r1r + 0.1875 * r2i, r1i - 0.1875 * r2r
            for m, s in enumerate((s1r, s1i, s2r, s2i, s3r, s3i)):
                out[pl.ds(32 * m + 8 * k, 8), here] = s
            return 0

        lax.fori_loop(0, 4, tile, 0)


def pack_kernel(own, other, fields, out):
    for k in range(6):
        s = own[32 * k : 32 * k + 32, :] + other[32 * k : 32 * k + 32, :]
        s = jnp.concatenate([s[:, 128 * c : 128 * c + 128] for c in range(4)], axis=0).T
        for c2 in range(2):
            out[pl.ds(2 * k + c2, 64, stride=17), :] = s[64 * c2 : 64 * c2 + 64]
    for c1 in range(4):
        out[pl.ds(12 + c1, 64, stride=17), :] = fields[pl.ds(c1, 64, stride=4), :]
    real = lax.broadcasted_iota(jnp.int32, (1, 128), 1) < 64
    g = own[192:194, :128] + other[192:194, :128]
    out[pl.ds(16, 64, stride=17), :] = jnp.broadcast_to(jnp.where(real, g[0:1], g[1:2]), (64, 128))


def columns_kernel(got, right, left, twiddle, wave, pre, out):
    def transform(xr, xi):
        yr, yi = cmul(xr, xi, pre[0], pre[1])
        y = split(jnp.concatenate([yr.T, yi.T], axis=0))
        o = mm3(y, (right[0], right[1]), ((1,), (0,)))
        ur = o[:128, :128] - o[128:, 128:]
        ui = o[:128, 128:] + o[128:, :128]
        vr, vi = cmul(ur, ui, twiddle[0], twiddle[1])
        v = split(jnp.concatenate([vr, vi], axis=1))
        o = mm3((left[0], left[1]), v, ((1,), (0,)))
        wr = o[:128, :128] - o[128:, 128:]
        wi = o[:128, 128:] + o[128:, :128]
        return cmul(wr, wi, wave[0], wave[1])

    x0, x1 = (
        jnp.concatenate([got[pl.ds(17 * f + 12 + c1, 32, stride=34), :] for c1 in range(4)], axis=0)
        for f in range(2)
    )
    low = lax.broadcasted_iota(jnp.int32, (128, 128), 1) < 64
    xr = jnp.where(low, x0, pltpu.roll(x1, 64, 1))
    xi = jnp.where(low, pltpu.roll(x0, 64, 1), x1)
    zr, zi = transform(xr, xi)
    for y in range(2):
        for f in range(2):
            for c2 in range(2):
                at = slice(64 * f + 32 * c2, 64 * f + 32 * c2 + 32)
                out[pl.ds(16 * y + 4 * f + c2, 32, stride=32), :] = zr[at]
                out[pl.ds(16 * y + 4 * f + 2 + c2, 32, stride=32), :] = zi[at]

    g = got[16:17, :] + got[33:34, :]
    gr, gi = g[:, 0:1], g[:, 64:65]

    def total(k):
        return jnp.concatenate(
            [
                got[pl.ds(2 * k + c2, 32, stride=34), :] + got[pl.ds(17 + 2 * k + c2, 32, stride=34), :]
                for c2 in range(2)
            ],
            axis=0,
        )

    s1r, s1i, s2r, s2i, s3r, s3i = (total(k) for k in range(6))
    er, ei, cr, ci = zr[:64], zi[:64], zr[64:], zi[64:]
    q = 0.03125 * (cr * cr + ci * ci)
    tr = s1r - q * s2r - (cr * s3i + ci * s3r) - (er * gi + ei * gr)
    ti = s1i - q * s2i + (cr * s3r - ci * s3i) + (er * gr - ei * gi)
    pr = er - 0.03125 * ti
    pi = ei + 0.03125 * tr
    zr, zi = transform(jnp.concatenate([pr, cr], axis=0), jnp.concatenate([pi, ci], axis=0))
    for y in range(2):
        for c1 in range(4):
            at = slice(32 * c1, 32 * c1 + 32)
            out[pl.ds(16 * y + 8 + c1, 32, stride=32), :] = zr[at]
            out[pl.ds(16 * y + 12 + c1, 32, stride=32), :] = zi[at]


def place(got, fields):
    for k in range(4):
        x = jnp.concatenate([got[pl.ds(2 * k + c2, 64, stride=16), :] for c2 in range(2)], axis=0).T
        for c1 in range(4):
            fields[k, :, 128 * c1 : 128 * c1 + 128] = x[32 * c1 : 32 * c1 + 32]


def half_step(part, rates, fields, a, b, gradient, a_out, b_out, a_buf, b_buf, sem):
    copies = []
    for k in range(4):
        rows = pl.ds(8 * k, 8)

        def tile(j, _, rows=rows):
            cols = pl.ds(pl.multiple_of(part * 512 + 128 * j, 128), 128)
            here = pl.ds(pl.multiple_of(128 * j, 128), 128)
            er, ei, cr, ci = (fields[m, rows, here] for m in range(4))
            d = gradient[rows, cols]
            d3 = 0.03125 * d
            q = 0.03125 * (cr * cr + ci * ci)
            wr, wi = d3 * cr - 0.215625 * ci, 0.215625 * cr + d3 * ci
            vr, vi = d3 * cr + 0.215625 * ci, 0.215625 * cr - d3 * ci
            lr = 0.9753125 - d3 * d - q
            li = -0.24375 * d
            yr = -0.03125 * (cr * er + ci * ei)
            yi = -0.03125 * (cr * ei - ci * er)
            fr, fi = -0.21875 * ei, 0.21875 * er
            for v in range(16):
                dv3, kr, ki = (rates[3 * v + m] for m in range(3))
                ar, ai = a[0, v, rows, cols], a[1, v, rows, cols]
                br, bi = b[0, v, rows, cols], b[1, v, rows, cols]
                mr = kr - q
                gr, gi = dv3 * cr, dv3 * ci
                ur, ui = wr + gr, wi + gi
                tr, ti = vr + gr, vi - gi
                a_buf[0, v, rows, here] = (mr * ar - ki * ai) + (ur * br - ui * bi) + (fr + dv3 * er)
                a_buf[1, v, rows, here] = (mr * ai + ki * ar) + (ur * bi + ui * br) + (fi + dv3 * ei)
                b_buf[0, v, rows, here] = (lr * br - li * bi) + (tr * ar - ti * ai) + yr
                b_buf[1, v, rows, here] = (lr * bi + li * br) + (tr * ai + ti * ar) + yi
            return 0

        lax.fori_loop(0, 4, tile, 0)
        cols = pl.ds(pl.multiple_of(part * 512, 128), 512)
        for n, (src, dst) in enumerate(((a_buf, a_out), (b_buf, b_out))):
            copy = pltpu.make_async_copy(src.at[:, :, rows, :], dst.at[:, :, rows, cols], sem.at[n, k])
            copy.start()
            copies.append(copy)
    return copies


def last_part(own, other, pre, table, twiddle, post, probe_out, control_out):
    zero = lax.axis_index("co") == 0
    x = []
    for k in range(4):
        parts = []
        for comp in range(2):
            pieces = []
            for h in range(2):
                for c1 in range(4):
                    at = pl.ds(16 * k + 8 + 4 * comp + c1, 16, stride=64)
                    mine, theirs = own[at, :], other[at, :]
                    pieces.append(jnp.where(zero, *((mine, theirs) if h == 0 else (theirs, mine))))
            z = jnp.concatenate(pieces, axis=0).T
            z = [jnp.concatenate([z[64 * f : 64 * f + 32], z[64 * f + 32 : 64 * f + 64]], axis=1) for f in range(2)]
            parts.append(jnp.concatenate(z, axis=0))
        x.extend(cmul(*parts, pre[k : k + 1, :], pre[4 + k : 5 + k, :]))
    o = mm3(split(jnp.concatenate(x, axis=0)), (table[0], table[1]), ((1,), (0,)))
    r, i = [], []
    for k in range(4):
        top, low = o[128 * k : 128 * k + 64], o[128 * k + 64 : 128 * k + 128]
        yr = top[:, :256] - low[:, 256:]
        yi = top[:, 256:] + low[:, :256]
        if k:
            yr, yi = cmul(yr, yi, twiddle[k : k + 1, :], twiddle[4 + k : 5 + k, :])
        r.append(yr)
        i.append(yi)
    r, i = butterfly(r, i)
    for k in range(4):
        at = slice(256 * k, 256 * k + 256)
        yr, yi = cmul(r[k], i[k], post[0:1, at], post[1:2, at])
        probe_out[0, :, at], probe_out[1, :, at] = yr[:32], yi[:32]
        control_out[0, :, at], control_out[1, :, at] = yr[32:], yi[32:]


def near_kernel(rates, got, a, b, gradient, a_out, b_out, fields, a_buf, b_buf, sem):
    place(got, fields)
    part = lax.axis_index("co")
    for copy in half_step(part, rates, fields, a, b, gradient, a_out, b_out, a_buf, b_buf, sem):
        copy.wait()


def far_kernel(
    rates, own, other, a, b, gradient, pre, table, twiddle, post, a_in, b_in,
    a_out, b_out, probe_out, control_out, fields, a_buf, b_buf, sem,
):
    del a_in, b_in
    place(other, fields)
    part = 1 - lax.axis_index("co")
    copies = half_step(part, rates, fields, a, b, gradient, a_out, b_out, a_buf, b_buf, sem)
    last_part(own, other, pre, table, twiddle, post, probe_out, control_out)
    for copy in copies:
        copy.wait()


VMEM = pl.BlockSpec(memory_space=pltpu.VMEM)


ANY = pl.BlockSpec(memory_space=pl.ANY)


def f32(*shape):
    return jax.ShapeDtypeStruct(shape, F32)


def near(*shape):
    return pltpu.VMEM(shape, F32)


def pinned(arrays):
    return [pltpu.with_memory_space_constraint(jnp.asarray(x), pltpu.VMEM) for x in arrays]


def far(arrays):
    return [pltpu.with_memory_space_constraint(jnp.asarray(x), pltpu.HBM) for x in arrays]


def limit(mib):
    return pltpu.CompilerParams(vmem_limit_bytes=mib << 20)


def shards(probe, control, optical, spin, doppler, weight, gradient):
    swap = [(0, 1), (1, 0)]
    tables = [jnp.asarray(t) for t in row_tables()]
    dma = pltpu.SemaphoreType.DMA
    state = optical.shape
    own, other, fields, optical, spin, gradient, rates = pl.pallas_call(
        front_kernel,
        out_shape=(near(200, 512), near(200, 512), near(256, 128), near(*state), near(*state), near(32, N), near(48, 8, 128)),
        in_specs=[ANY] * 11,
        out_specs=(VMEM,) * 7,
        scratch_shapes=[
            pltpu.VMEM((2, 32, N), F32),
            *(pltpu.VMEM(t.shape, t.dtype) for t in tables),
            pltpu.SMEM((16,), F32),
            pltpu.SMEM((16,), F32),
            dma((2, 8)),
            dma((8,)),
        ],
        compiler_params=limit(6),
        name="front",
    )(*far([doppler, weight, optical, spin, probe, control, gradient, *tables]))
    other = lax.ppermute(other, "co", swap)
    message = pl.pallas_call(
        pack_kernel,
        out_shape=near(17 * 64, 128),
        in_specs=[VMEM] * 3,
        out_specs=VMEM,
        compiler_params=limit(6),
        name="pack",
    )(*pinned([own, other, fields]))

    def exchange(x):
        shape = x.shape
        x = lax.all_to_all(x.reshape(64, -1, 1, 128), ("space", "yh"), 0, 0, tiled=True)
        return x.reshape(shape)

    tables = column_tables()
    message = pl.pallas_call(
        columns_kernel,
        out_shape=near(N, 128),
        in_specs=[VMEM] * (1 + len(tables)),
        out_specs=VMEM,
        compiler_params=limit(6),
        name="columns",
    )(*pinned([exchange(message), *tables]))
    got = exchange(message)
    other = lax.ppermute(got, "co", swap)
    scratch = [
        pltpu.VMEM((4, 32, 512), F32),
        pltpu.VMEM((2, 16, 32, 512), F32),
        pltpu.VMEM((2, 16, 32, 512), F32),
        dma((2, 4)),
    ]
    halfway = pl.pallas_call(
        near_kernel,
        out_shape=(f32(*state), f32(*state)),
        in_specs=[VMEM] * 5,
        out_specs=(ANY, ANY),
        scratch_shapes=scratch,
        compiler_params=limit(8),
        name="near",
    )(*pinned([rates, got, optical, spin, gradient]))
    tables = last_tables()
    optical, spin, probe, control = pl.pallas_call(
        far_kernel,
        out_shape=(f32(*state), f32(*state), f32(2, 32, N), f32(2, 32, N)),
        in_specs=[VMEM] * (6 + len(tables)) + [ANY] * 2,
        out_specs=(ANY, ANY, VMEM, VMEM),
        scratch_shapes=scratch,
        input_output_aliases={10: 0, 11: 1},
        compiler_params=limit(12),
        name="far",
    )(*pinned([rates, got, other, optical, spin, gradient, *tables]), *halfway)
    return probe, control, optical, spin


def solution(mesh):
    fine = Mesh(mesh.devices.reshape(mesh.devices.shape[0], 2, 2), ("space", "yh", "co"))
    vel = ("yh", "co")
    field, state = P(None, "space", None), P(None, vel, "space", None)
    return jax.shard_map(
        shards,
        mesh=fine,
        in_specs=(field, field, state, state, P(vel), P(vel), P("space", None)),
        out_specs=(field, field, state, state),
        check_vma=False,
    )
```

```python
import jax
import jax.numpy as jnp
import numpy as np
from jax import lax
from jax.experimental import pallas as pl
from jax.experimental.pallas import tpu as pltpu
from jax.sharding import Mesh
from jax.sharding import PartitionSpec as P


N = 1024
BF16 = jnp.bfloat16
F32 = jnp.float32


def turn(numerator, period):
    angle = 2.0 * np.pi * (np.asarray(numerator, np.int64) % period) / period
    return np.cos(angle) + 1j * np.sin(angle)


NORM = np.exp(-0.25j * np.pi) / 32.0


def chirp(n):
    return turn(np.asarray(n, np.int64) ** 2, 2 * N)


def pair(z):
    return np.stack([z.real, z.imag]).astype(np.float32)


def halves(x):
    x = np.asarray(x, np.float32)
    high = x.astype(BF16)
    low = (x - high.astype(np.float32)).astype(BF16)
    return np.stack([high, low])


def row_tables():
    n = np.arange(N)
    pre = pair(NORM * chirp(n))
    short = np.arange(256)
    twiddle = pair(turn(-np.arange(4)[:, None] * short[None, :], N)).reshape(8, 256)
    dft = turn(-np.arange(128)[:, None] * short[None, :], 256)
    table = halves(np.concatenate([dft.real, dft.imag], axis=0))
    out = 4 * np.arange(128)[:, None] + np.repeat(np.arange(4), 32)[None, :]
    return pre, twiddle, table, pair(chirp(out))


def column_tables():
    eye = np.eye(4)
    small = turn(-np.arange(32)[:, None] * np.arange(32)[None, :], 32)
    norm = NORM * small
    right = np.concatenate([np.kron(eye, norm.real), np.kron(eye, norm.imag)], axis=1)
    left = np.concatenate([np.kron(eye, small.real), np.kron(eye, small.imag)], axis=0)
    outer, inner = np.arange(32)[:, None], np.tile(np.arange(32), 4)[None, :]
    return halves(right), halves(left), pair(turn(-outer * inner, N)), pair(chirp(32 * outer + inner))


def last_tables():
    c2, h, c1, t = np.meshgrid(np.arange(2), np.arange(2), np.arange(4), np.arange(16), indexing="ij")
    quarter = (128 * h + 16 * (2 * c1 + c2) + t).reshape(-1)
    classes = np.arange(4)
    pre = pair(NORM * chirp(4 * quarter[None, :] + classes[:, None])).reshape(8, 256)
    short = np.arange(256)
    dft = turn(-quarter[:, None] * short[None, :], 256)
    table = halves(np.concatenate([dft.real, dft.imag], axis=1))
    twiddle = pair(turn(-classes[:, None] * short[None, :], N)).reshape(8, 256)
    return pre, table, twiddle, pair(chirp(np.arange(N)))


def split(x):
    high = x.astype(BF16)
    return high, (x - high.astype(F32)).astype(BF16)


def mm(a, b, dims):
    return lax.dot_general(a, b, (dims, ((), ())), preferred_element_type=F32)


def mm3(a, b, dims):
    (ah, al), (bh, bl) = a, b
    return mm(ah, bh, dims) + (mm(ah, bl, dims) + mm(al, bh, dims))


def cmul(xr, xi, yr, yi):
    return xr * yr - xi * yi, xr * yi + xi * yr


def butterfly(r, i):
    ar, ai, br, bi = r[0] + r[2], i[0] + i[2], r[0] - r[2], i[0] - i[2]
    cr, ci, dr, di = r[1] + r[3], i[1] + i[3], r[1] - r[3], i[1] - i[3]
    return (
        [ar + cr, br + di, ar - cr, br - di],
        [ai + ci, bi - dr, ai - ci, bi + dr],
    )


def rows_part(x, core, pre, twiddle, table, post, out):
    lane = lax.broadcasted_iota(jnp.int32, (1, N), 1)
    sign = jnp.where((lane & core) == 1, -1.0, 1.0)
    xr, xi = cmul(x[0], x[1], pre[0:1, :] * sign, pre[1:2, :] * sign)
    r, i = butterfly(
        [xr[:, 256 * k : 256 * k + 256] for k in range(4)],
        [xi[:, 256 * k : 256 * k + 256] for k in range(4)],
    )
    for p in range(1, 4):
        r[p], i[p] = cmul(r[p], i[p], twiddle[p : p + 1, :], twiddle[4 + p : 5 + p, :])
    x = split(jnp.concatenate(r + i, axis=0))
    o = mm3((table[0], table[1]), x, ((1,), (1,)))
    yr = o[:128, :128] - o[128:, 128:]
    yi = o[:128, 128:] + o[128:, :128]
    lane = lax.broadcasted_iota(jnp.int32, (1, 128), 1)
    sign = jnp.where(((lane // 32) & core) == 1, -1.0, 1.0)
    yr, yi = cmul(yr, yi, post[0] * sign, post[1] * sign)
    for c1 in range(4):
        for p in range(4):
            piece = [
                y[16 * (2 * c1 + c2) : 16 * (2 * c1 + c2) + 16, 32 * p : 32 * p + 32]
                for y in (yr, yi)
                for c2 in range(2)
            ]
            out[pl.ds(4 * p + c1, 16, stride=16), :] = jnp.concatenate(piece, axis=1)


def front_kernel(
    doppler_hbm, weight_hbm, a_hbm, b_hbm, probe, control, gradient_hbm, pre_hbm, twiddle_hbm, table_hbm, post_hbm,
    own, other, fields, a, b, gradient, rates, x, pre, twiddle, table, post, doppler, weight, state_sem, sem,
):
    core, half = lax.axis_index("co"), lax.axis_index("yh")
    small = [
        pltpu.make_async_copy(src, dst, sem.at[k])
        for k, (src, dst) in enumerate(
            (
                (pre_hbm, pre),
                (twiddle_hbm, twiddle),
                (table_hbm, table),
                (post_hbm, post),
                (gradient_hbm, gradient),
                (doppler_hbm, doppler),
                (weight_hbm, weight),
            )
        )
    ]

    @pl.when(half == 0)
    def _():
        pltpu.make_async_copy(probe, x, sem.at[7]).start()

    @pl.when(half == 1)
    def _():
        pltpu.make_async_copy(control, x, sem.at[7]).start()

    for copy in small:
        copy.start()

    def chunk(n):
        rows = pl.ds(8 * (n // 2), 8)
        cols = pl.ds(pl.multiple_of((core if n % 2 else 1 - core) * 512, 512), 512)
        return [
            pltpu.make_async_copy(src.at[:, :, rows, cols], dst.at[:, :, rows, cols], state_sem.at[m, n])
            for m, (src, dst) in enumerate(((a_hbm, a), (b_hbm, b)))
        ]

    def start(n):
        for copy in chunk(n):
            copy.start()

    ahead = 4
    for n in range(ahead):
        start(n)

    pltpu.make_async_copy(probe, x, sem.at[7]).wait()
    for copy in small:
        copy.wait()
    rows_part(x, core, pre, twiddle, table, post, fields)
    gr, gi = 0.0, 0.0
    for v in range(16):
        gr = gr + weight[v]
        gi = gi + weight[v] * doppler[v]
    first = lax.broadcasted_iota(jnp.int32, (8, 512), 0) == 0
    for out in (own, other):
        out[192:200, :] = jnp.where(first, 0.21875 * gr, -0.03125 * gi)
    for v in range(16):
        d = doppler[v]
        for m, c in enumerate((0.03125 * d, 0.78125 - 0.03125 * d * d, -0.1875 * d)):
            rates[3 * v + m] = jnp.full((8, 128), c, F32)

    for n in range(8):
        for copy in chunk(n):
            copy.wait()
        if n + ahead < 8:
            start(n + ahead)
        k = n // 2
        rows = pl.ds(8 * k, 8)
        out, part = (own, core) if n % 2 else (other, 1 - core)

        def tile(j, _, out=out, part=part, rows=rows, k=k):
            cols = pl.ds(pl.multiple_of(part * 512 + 128 * j, 128), 128)
            here = pl.ds(pl.multiple_of(128 * j, 128), 128)
            acc = None
            for v in range(16):
                d, w = doppler[v], weight[v]
                wd = w * d
                w1 = w * (0.78125 - 0.03125 * d * d)
                ar, ai = a[0, v, rows, cols], a[1, v, rows, cols]
                br, bi = b[0, v, rows, cols], b[1, v, rows, cols]
                new = (
                    w1 * ar, w1 * ai, wd * ar, wd * ai, w * ar, w * ai,
                    w * br, w * bi, wd * br, wd * bi,
                )
                acc = new if acc is None else tuple(x + y for x, y in zip(acc, new))
            r1r, r1i, r2r, r2i, s2r, s2i, s4r, s4i, t4r, t4i = acc
            g = 0.03125 * gradient[rows, cols]
            s3r = 0.215625 * s4r + 0.03125 * t4i + g * s4i
            s3i = 0.215625 * s4i - 0.03125 * t4r - g * s4r
            s1r, s1i = r1r + 0.1875 * r2i, r1i - 0.1875 * r2r
            for m, s in enumerate((s1r, s1i, s2r, s2i, s3r, s3i)):
                out[pl.ds(32 * m + 8 * k, 8), here] = s
            return 0

        lax.fori_loop(0, 4, tile, 0)


def pack_kernel(own, other, fields, out):
    for k in range(6):
        s = own[32 * k : 32 * k + 32, :] + other[32 * k : 32 * k + 32, :]
        s = jnp.concatenate([s[:, 128 * c : 128 * c + 128] for c in range(4)], axis=0).T
        for c2 in range(2):
            out[pl.ds(2 * k + c2, 64, stride=17), :] = s[64 * c2 : 64 * c2 + 64]
    for c1 in range(4):
        out[pl.ds(12 + c1, 64, stride=17), :] = fields[pl.ds(c1, 64, stride=4), :]
    real = lax.broadcasted_iota(jnp.int32, (1, 128), 1) < 64
    g = own[192:194, :128] + other[192:194, :128]
    out[pl.ds(16, 64, stride=17), :] = jnp.broadcast_to(jnp.where(real, g[0:1], g[1:2]), (64, 128))


def columns_kernel(got, right, left, twiddle, wave, out):
    twiddle, wave = ([jnp.concatenate([t[k]] * 4, axis=0) for k in range(2)] for t in (twiddle, wave))

    def transform(xr, xi):
        yr, yi = cmul(xr, xi, wave[0], wave[1])
        y = split(jnp.concatenate([yr.T, yi.T], axis=0))
        o = mm3(y, (right[0], right[1]), ((1,), (0,)))
        ur = o[:128, :128] - o[128:, 128:]
        ui = o[:128, 128:] + o[128:, :128]
        vr, vi = cmul(ur, ui, twiddle[0], twiddle[1])
        v = split(jnp.concatenate([vr, vi], axis=1))
        o = mm3((left[0], left[1]), v, ((1,), (0,)))
        wr = o[:128, :128] - o[128:, 128:]
        wi = o[:128, 128:] + o[128:, :128]
        return cmul(wr, wi, wave[0], wave[1])

    x0, x1 = (
        jnp.concatenate([got[pl.ds(17 * f + 12 + c1, 32, stride=34), :] for c1 in range(4)], axis=0)
        for f in range(2)
    )
    low = lax.broadcasted_iota(jnp.int32, (128, 128), 1) < 64
    xr = jnp.where(low, x0, pltpu.roll(x1, 64, 1))
    xi = jnp.where(low, pltpu.roll(x0, 64, 1), x1)
    zr, zi = transform(xr, xi)
    for y in range(2):
        for f in range(2):
            for c2 in range(2):
                at = slice(64 * f + 32 * c2, 64 * f + 32 * c2 + 32)
                out[pl.ds(16 * y + 4 * f + c2, 32, stride=32), :] = zr[at]
                out[pl.ds(16 * y + 4 * f + 2 + c2, 32, stride=32), :] = zi[at]

    g = got[16:17, :] + got[33:34, :]
    gr, gi = g[:, 0:1], g[:, 64:65]

    def total(k):
        return jnp.concatenate(
            [
                got[pl.ds(2 * k + c2, 32, stride=34), :] + got[pl.ds(17 + 2 * k + c2, 32, stride=34), :]
                for c2 in range(2)
            ],
            axis=0,
        )

    s1r, s1i, s2r, s2i, s3r, s3i = (total(k) for k in range(6))
    er, ei, cr, ci = zr[:64], zi[:64], zr[64:], zi[64:]
    q = 0.03125 * (cr * cr + ci * ci)
    tr = s1r - q * s2r - (cr * s3i + ci * s3r) - (er * gi + ei * gr)
    ti = s1i - q * s2i + (cr * s3r - ci * s3i) + (er * gr - ei * gi)
    pr = er - 0.03125 * ti
    pi = ei + 0.03125 * tr
    zr, zi = transform(jnp.concatenate([pr, cr], axis=0), jnp.concatenate([pi, ci], axis=0))
    for y in range(2):
        for c1 in range(4):
            at = slice(32 * c1, 32 * c1 + 32)
            out[pl.ds(16 * y + 8 + c1, 32, stride=32), :] = zr[at]
            out[pl.ds(16 * y + 12 + c1, 32, stride=32), :] = zi[at]


def place(got, fields):
    for k in range(4):
        x = jnp.concatenate([got[pl.ds(2 * k + c2, 64, stride=16), :] for c2 in range(2)], axis=0).T
        for c1 in range(4):
            fields[k, :, 128 * c1 : 128 * c1 + 128] = x[32 * c1 : 32 * c1 + 32]


def half_step(part, rates, fields, a, b, gradient, a_out, b_out, a_buf, b_buf, sem):
    copies = []
    for k in range(4):
        rows = pl.ds(8 * k, 8)

        def tile(j, _, rows=rows):
            cols = pl.ds(pl.multiple_of(part * 512 + 128 * j, 128), 128)
            here = pl.ds(pl.multiple_of(128 * j, 128), 128)
            er, ei, cr, ci = (fields[m, rows, here] for m in range(4))
            d = gradient[rows, cols]
            d3 = 0.03125 * d
            q = 0.03125 * (cr * cr + ci * ci)
            wr, wi = d3 * cr - 0.215625 * ci, 0.215625 * cr + d3 * ci
            vr, vi = d3 * cr + 0.215625 * ci, 0.215625 * cr - d3 * ci
            lr = 0.9753125 - d3 * d - q
            li = -0.24375 * d
            yr = -0.03125 * (cr * er + ci * ei)
            yi = -0.03125 * (cr * ei - ci * er)
            fr, fi = -0.21875 * ei, 0.21875 * er
            for v in range(16):
                dv3, kr, ki = (rates[3 * v + m] for m in range(3))
                ar, ai = a[0, v, rows, cols], a[1, v, rows, cols]
                br, bi = b[0, v, rows, cols], b[1, v, rows, cols]
                mr = kr - q
                gr, gi = dv3 * cr, dv3 * ci
                ur, ui = wr + gr, wi + gi
                tr, ti = vr + gr, vi - gi
                a_buf[0, v, rows, here] = (mr * ar - ki * ai) + (ur * br - ui * bi) + (fr + dv3 * er)
                a_buf[1, v, rows, here] = (mr * ai + ki * ar) + (ur * bi + ui * br) + (fi + dv3 * ei)
                b_buf[0, v, rows, here] = (lr * br - li * bi) + (tr * ar - ti * ai) + yr
                b_buf[1, v, rows, here] = (lr * bi + li * br) + (tr * ai + ti * ar) + yi
            return 0

        lax.fori_loop(0, 4, tile, 0)
        cols = pl.ds(pl.multiple_of(part * 512, 128), 512)
        for n, (src, dst) in enumerate(((a_buf, a_out), (b_buf, b_out))):
            copy = pltpu.make_async_copy(src.at[:, :, rows, :], dst.at[:, :, rows, cols], sem.at[n, k])
            copy.start()
            copies.append(copy)
    return copies


def last_part(own, other, pre, table, twiddle, post, probe_out, control_out):
    zero = lax.axis_index("co") == 0
    x = []
    for k in range(4):
        parts = []
        for comp in range(2):
            pieces = []
            for h in range(2):
                for c1 in range(4):
                    at = pl.ds(16 * k + 8 + 4 * comp + c1, 16, stride=64)
                    mine, theirs = own[at, :], other[at, :]
                    pieces.append(jnp.where(zero, *((mine, theirs) if h == 0 else (theirs, mine))))
            z = jnp.concatenate(pieces, axis=0).T
            z = [jnp.concatenate([z[64 * f : 64 * f + 32], z[64 * f + 32 : 64 * f + 64]], axis=1) for f in range(2)]
            parts.append(jnp.concatenate(z, axis=0))
        x.extend(cmul(*parts, pre[k : k + 1, :], pre[4 + k : 5 + k, :]))
    o = mm3(split(jnp.concatenate(x, axis=0)), (table[0], table[1]), ((1,), (0,)))
    r, i = [], []
    for k in range(4):
        top, low = o[128 * k : 128 * k + 64], o[128 * k + 64 : 128 * k + 128]
        yr = top[:, :256] - low[:, 256:]
        yi = top[:, 256:] + low[:, :256]
        if k:
            yr, yi = cmul(yr, yi, twiddle[k : k + 1, :], twiddle[4 + k : 5 + k, :])
        r.append(yr)
        i.append(yi)
    r, i = butterfly(r, i)
    for k in range(4):
        at = slice(256 * k, 256 * k + 256)
        yr, yi = cmul(r[k], i[k], post[0:1, at], post[1:2, at])
        probe_out[0, :, at], probe_out[1, :, at] = yr[:32], yi[:32]
        control_out[0, :, at], control_out[1, :, at] = yr[32:], yi[32:]


def near_kernel(rates, got, a, b, gradient, a_out, b_out, fields, a_buf, b_buf, sem):
    place(got, fields)
    part = lax.axis_index("co")
    for copy in half_step(part, rates, fields, a, b, gradient, a_out, b_out, a_buf, b_buf, sem):
        copy.wait()


def far_kernel(
    rates, own, other, a, b, gradient, pre, table, twiddle, post, a_in, b_in,
    a_out, b_out, probe_out, control_out, fields, a_buf, b_buf, sem, probe_buf, control_buf, last_sem,
):
    del a_in, b_in
    place(other, fields)
    part = 1 - lax.axis_index("co")
    copies = half_step(part, rates, fields, a, b, gradient, a_out, b_out, a_buf, b_buf, sem)
    last_part(own, other, pre, table, twiddle, post, probe_buf, control_buf)
    for k, (src, dst) in enumerate(((probe_buf, probe_out), (control_buf, control_out))):
        copies.append(pltpu.make_async_copy(src, dst, last_sem.at[k]))
        copies[-1].start()
    for copy in copies:
        copy.wait()


VMEM = pl.BlockSpec(memory_space=pltpu.VMEM)


ANY = pl.BlockSpec(memory_space=pl.ANY)


def f32(*shape):
    return jax.ShapeDtypeStruct(shape, F32)


def near(*shape):
    return pltpu.VMEM(shape, F32)


def pinned(arrays):
    return [pltpu.with_memory_space_constraint(jnp.asarray(x), pltpu.VMEM) for x in arrays]


def far(arrays):
    return [pltpu.with_memory_space_constraint(jnp.asarray(x), pltpu.HBM) for x in arrays]


def limit(mib):
    return pltpu.CompilerParams(vmem_limit_bytes=mib << 20)


def shards(probe, control, optical, spin, doppler, weight, gradient):
    swap = [(0, 1), (1, 0)]
    tables = [jnp.asarray(t) for t in row_tables()]
    dma = pltpu.SemaphoreType.DMA
    state = optical.shape
    own, other, fields, optical, spin, gradient, rates = pl.pallas_call(
        front_kernel,
        out_shape=(near(200, 512), near(200, 512), near(256, 128), near(*state), near(*state), near(32, N), near(48, 8, 128)),
        in_specs=[ANY] * 11,
        out_specs=(VMEM,) * 7,
        scratch_shapes=[
            pltpu.VMEM((2, 32, N), F32),
            *(pltpu.VMEM(t.shape, t.dtype) for t in tables),
            pltpu.SMEM((16,), F32),
            pltpu.SMEM((16,), F32),
            dma((2, 8)),
            dma((8,)),
        ],
        compiler_params=limit(6),
        name="front",
    )(*far([doppler, weight, optical, spin, probe, control, gradient, *tables]))
    other = lax.ppermute(other, "co", swap)
    message = pl.pallas_call(
        pack_kernel,
        out_shape=near(17 * 64, 128),
        in_specs=[VMEM] * 3,
        out_specs=VMEM,
        compiler_params=limit(6),
        name="pack",
    )(*pinned([own, other, fields]))

    def exchange(x):
        shape = x.shape
        x = lax.all_to_all(x.reshape(64, -1, 1, 128), ("space", "yh"), 0, 0, tiled=True)
        return x.reshape(shape)

    tables = column_tables()
    message = pl.pallas_call(
        columns_kernel,
        out_shape=near(N, 128),
        in_specs=[VMEM] * (1 + len(tables)),
        out_specs=VMEM,
        compiler_params=limit(6),
        name="columns",
    )(*pinned([exchange(message), *tables]))
    got = exchange(message)
    other = lax.ppermute(got, "co", swap)
    scratch = [
        pltpu.VMEM((4, 32, 512), F32),
        pltpu.VMEM((2, 16, 32, 512), F32),
        pltpu.VMEM((2, 16, 32, 512), F32),
        dma((2, 4)),
    ]
    halfway = pl.pallas_call(
        near_kernel,
        out_shape=(f32(*state), f32(*state)),
        in_specs=[VMEM] * 5,
        out_specs=(ANY, ANY),
        scratch_shapes=scratch,
        compiler_params=limit(8),
        name="near",
    )(*pinned([rates, got, optical, spin, gradient]))
    tables = last_tables()
    optical, spin, probe, control = pl.pallas_call(
        far_kernel,
        out_shape=(f32(*state), f32(*state), f32(2, 32, N), f32(2, 32, N)),
        in_specs=[VMEM] * (6 + len(tables)) + [ANY] * 2,
        out_specs=(ANY,) * 4,
        scratch_shapes=scratch + [pltpu.VMEM((2, 32, N), F32), pltpu.VMEM((2, 32, N), F32), dma((2,))],
        input_output_aliases={10: 0, 11: 1},
        compiler_params=limit(12),
        name="far",
    )(*pinned([rates, got, other, optical, spin, gradient, *tables]), *halfway)
    return probe, control, optical, spin


def solution(mesh):
    fine = Mesh(mesh.devices.reshape(mesh.devices.shape[0], 2, 2), ("space", "yh", "co"))
    vel = ("yh", "co")
    field, state = P(None, "space", None), P(None, vel, "space", None)
    return jax.shard_map(
        shards,
        mesh=fine,
        in_specs=(field, field, state, state, P(vel), P(vel), P("space", None)),
        out_specs=(field, field, state, state),
        check_vma=False,
    )
```

```python
import jax
import jax.numpy as jnp
import numpy as np
from jax import lax
from jax.experimental import pallas as pl
from jax.experimental.pallas import tpu as pltpu
from jax.sharding import Mesh
from jax.sharding import PartitionSpec as P


N = 1024
BF16 = jnp.bfloat16
F32 = jnp.float32


def turn(numerator, period):
    angle = 2.0 * np.pi * (np.asarray(numerator, np.int64) % period) / period
    return np.cos(angle) + 1j * np.sin(angle)


NORM = np.exp(-0.25j * np.pi) / 32.0


def chirp(n):
    return turn(np.asarray(n, np.int64) ** 2, 2 * N)


def pair(z):
    return np.stack([z.real, z.imag]).astype(np.float32)


def halves(x):
    x = np.asarray(x, np.float32)
    high = x.astype(BF16)
    low = (x - high.astype(np.float32)).astype(BF16)
    return np.stack([high, low])


def row_tables():
    n = np.arange(N)
    pre = pair(NORM * chirp(n))
    short = np.arange(256)
    twiddle = pair(turn(-np.arange(4)[:, None] * short[None, :], N)).reshape(8, 256)
    dft = turn(-np.arange(128)[:, None] * short[None, :], 256)
    table = halves(np.concatenate([dft.real, dft.imag], axis=0))
    out = 4 * np.arange(128)[:, None] + np.repeat(np.arange(4), 32)[None, :]
    return pre, twiddle, table, pair(chirp(out))


def column_tables():
    eye = np.eye(4)
    small = turn(-np.arange(32)[:, None] * np.arange(32)[None, :], 32)
    norm = NORM * small
    right, turned = (np.concatenate([np.kron(eye, f.real), np.kron(eye, f.imag)], axis=1) for f in (norm, 1j * norm))
    right = np.concatenate([right, turned], axis=0)
    left, turned = (np.concatenate([np.kron(eye, f.real), np.kron(eye, f.imag)], axis=0) for f in (small, 1j * small))
    left = np.concatenate([left, turned], axis=1)
    outer, inner = np.arange(32)[:, None], np.tile(np.arange(32), 4)[None, :]
    return halves(right), halves(left), pair(turn(-outer * inner, N)), pair(chirp(32 * outer + inner))


def last_tables():
    c2, h, c1, t = np.meshgrid(np.arange(2), np.arange(2), np.arange(4), np.arange(16), indexing="ij")
    quarter = (128 * h + 16 * (2 * c1 + c2) + t).reshape(-1)
    classes = np.arange(4)
    pre = pair(NORM * chirp(4 * quarter[None, :] + classes[:, None])).reshape(8, 256)
    short = np.arange(256)
    dft = turn(-quarter[:, None] * short[None, :], 256)
    table = halves(np.concatenate([dft.real, dft.imag], axis=1))
    twiddle = pair(turn(-classes[:, None] * short[None, :], N)).reshape(8, 256)
    return pre, table, twiddle, pair(chirp(np.arange(N)))


def split(x):
    high = x.astype(BF16)
    return high, (x - high.astype(F32)).astype(BF16)


def mm(a, b, dims):
    return lax.dot_general(a, b, (dims, ((), ())), preferred_element_type=F32)


def mm3(a, b, dims):
    (ah, al), (bh, bl) = a, b
    return mm(ah, bh, dims) + (mm(ah, bl, dims) + mm(al, bh, dims))


def cmul(xr, xi, yr, yi):
    return xr * yr - xi * yi, xr * yi + xi * yr


def butterfly(r, i):
    ar, ai, br, bi = r[0] + r[2], i[0] + i[2], r[0] - r[2], i[0] - i[2]
    cr, ci, dr, di = r[1] + r[3], i[1] + i[3], r[1] - r[3], i[1] - i[3]
    return (
        [ar + cr, br + di, ar - cr, br - di],
        [ai + ci, bi - dr, ai - ci, bi + dr],
    )


def rows_part(x, core, pre, twiddle, table, post, out):
    lane = lax.broadcasted_iota(jnp.int32, (1, N), 1)
    sign = jnp.where((lane & core) == 1, -1.0, 1.0)
    xr, xi = cmul(x[0], x[1], pre[0:1, :] * sign, pre[1:2, :] * sign)
    r, i = butterfly(
        [xr[:, 256 * k : 256 * k + 256] for k in range(4)],
        [xi[:, 256 * k : 256 * k + 256] for k in range(4)],
    )
    for p in range(1, 4):
        r[p], i[p] = cmul(r[p], i[p], twiddle[p : p + 1, :], twiddle[4 + p : 5 + p, :])
    x = split(jnp.concatenate(r + i, axis=0))
    o = mm3((table[0], table[1]), x, ((1,), (1,)))
    yr = o[:128, :128] - o[128:, 128:]
    yi = o[:128, 128:] + o[128:, :128]
    lane = lax.broadcasted_iota(jnp.int32, (1, 128), 1)
    sign = jnp.where(((lane // 32) & core) == 1, -1.0, 1.0)
    yr, yi = cmul(yr, yi, post[0] * sign, post[1] * sign)
    for c1 in range(4):
        for p in range(4):
            piece = [
                y[16 * (2 * c1 + c2) : 16 * (2 * c1 + c2) + 16, 32 * p : 32 * p + 32]
                for y in (yr, yi)
                for c2 in range(2)
            ]
            out[pl.ds(4 * p + c1, 16, stride=16), :] = jnp.concatenate(piece, axis=1)


def front_kernel(
    doppler_hbm, weight_hbm, a_hbm, b_hbm, probe, control, gradient_hbm, pre_hbm, twiddle_hbm, table_hbm, post_hbm,
    own, other, fields, a, b, gradient, rates, x, pre, twiddle, table, post, doppler, weight, state_sem, sem,
):
    core, half = lax.axis_index("co"), lax.axis_index("yh")
    small = [
        pltpu.make_async_copy(src, dst, sem.at[k])
        for k, (src, dst) in enumerate(
            (
                (pre_hbm, pre),
                (twiddle_hbm, twiddle),
                (table_hbm, table),
                (post_hbm, post),
                (gradient_hbm, gradient),
                (doppler_hbm, doppler),
                (weight_hbm, weight),
            )
        )
    ]

    @pl.when(half == 0)
    def _():
        pltpu.make_async_copy(probe, x, sem.at[7]).start()

    @pl.when(half == 1)
    def _():
        pltpu.make_async_copy(control, x, sem.at[7]).start()

    for copy in small:
        copy.start()

    def chunk(n):
        rows = pl.ds(8 * (n // 2), 8)
        cols = pl.ds(pl.multiple_of((core if n % 2 else 1 - core) * 512, 512), 512)
        return [
            pltpu.make_async_copy(src.at[:, :, rows, cols], dst.at[:, :, rows, cols], state_sem.at[m, n])
            for m, (src, dst) in enumerate(((a_hbm, a), (b_hbm, b)))
        ]

    def start(n):
        for copy in chunk(n):
            copy.start()

    ahead = 4
    for n in range(ahead):
        start(n)

    pltpu.make_async_copy(probe, x, sem.at[7]).wait()
    for copy in small:
        copy.wait()
    rows_part(x, core, pre, twiddle, table, post, fields)
    gr, gi = 0.0, 0.0
    for v in range(16):
        gr = gr + weight[v]
        gi = gi + weight[v] * doppler[v]
    first = lax.broadcasted_iota(jnp.int32, (8, 512), 0) == 0
    for out in (own, other):
        out[192:200, :] = jnp.where(first, 0.21875 * gr, -0.03125 * gi)
    for v in range(16):
        d = doppler[v]
        for m, c in enumerate((0.03125 * d, 0.78125 - 0.03125 * d * d, -0.1875 * d)):
            rates[3 * v + m] = jnp.full((8, 128), c, F32)

    for n in range(8):
        for copy in chunk(n):
            copy.wait()
        if n + ahead < 8:
            start(n + ahead)
        k = n // 2
        rows = pl.ds(8 * k, 8)
        out, part = (own, core) if n % 2 else (other, 1 - core)

        def tile(j, _, out=out, part=part, rows=rows, k=k):
            cols = pl.ds(pl.multiple_of(part * 512 + 128 * j, 128), 128)
            here = pl.ds(pl.multiple_of(128 * j, 128), 128)
            acc = None
            for v in range(16):
                d, w = doppler[v], weight[v]
                wd = w * d
                w1 = w * (0.78125 - 0.03125 * d * d)
                ar, ai = a[0, v, rows, cols], a[1, v, rows, cols]
                br, bi = b[0, v, rows, cols], b[1, v, rows, cols]
                new = (
                    w1 * ar, w1 * ai, wd * ar, wd * ai, w * ar, w * ai,
                    w * br, w * bi, wd * br, wd * bi,
                )
                acc = new if acc is None else tuple(x + y for x, y in zip(acc, new))
            r1r, r1i, r2r, r2i, s2r, s2i, s4r, s4i, t4r, t4i = acc
            g = 0.03125 * gradient[rows, cols]
            s3r = 0.215625 * s4r + 0.03125 * t4i + g * s4i
            s3i = 0.215625 * s4i - 0.03125 * t4r - g * s4r
            s1r, s1i = r1r + 0.1875 * r2i, r1i - 0.1875 * r2r
            for m, s in enumerate((s1r, s1i, s2r, s2i, s3r, s3i)):
                out[pl.ds(32 * m + 8 * k, 8), here] = s
            return 0

        lax.fori_loop(0, 4, tile, 0)


def pack_kernel(own, other, fields, out):
    for k in range(6):
        s = own[32 * k : 32 * k + 32, :] + other[32 * k : 32 * k + 32, :]
        s = jnp.concatenate([s[:, 128 * c : 128 * c + 128] for c in range(4)], axis=0).T
        for c2 in range(2):
            out[pl.ds(2 * k + c2, 64, stride=17), :] = s[64 * c2 : 64 * c2 + 64]
    for c1 in range(4):
        out[pl.ds(12 + c1, 64, stride=17), :] = fields[pl.ds(c1, 64, stride=4), :]
    real = lax.broadcasted_iota(jnp.int32, (1, 128), 1) < 64
    g = own[192:194, :128] + other[192:194, :128]
    out[pl.ds(16, 64, stride=17), :] = jnp.broadcast_to(jnp.where(real, g[0:1], g[1:2]), (64, 128))


def columns_kernel(got, right, left, twiddle, wave, out):
    twiddle, wave = ([jnp.concatenate([t[k]] * 4, axis=0) for k in range(2)] for t in (twiddle, wave))

    def transform(xr, xi):
        yr, yi = cmul(xr, xi, wave[0], wave[1])
        y = split(jnp.concatenate([yr.T, yi.T], axis=1))
        o = mm3(y, (right[0], right[1]), ((1,), (0,)))
        vr, vi = cmul(o[:, :128], o[:, 128:], twiddle[0], twiddle[1])
        high, low = split(jnp.concatenate([vr, vi], axis=0))
        o = mm(left[0], jnp.concatenate([high, low], axis=1), ((1,), (0,)))
        o = o[:, :128] + (o[:, 128:] + mm(left[1], high, ((1,), (0,))))
        wr, wi = o[:128], o[128:]
        return cmul(wr, wi, wave[0], wave[1])

    x0, x1 = (
        jnp.concatenate([got[pl.ds(17 * f + 12 + c1, 32, stride=34), :] for c1 in range(4)], axis=0)
        for f in range(2)
    )
    low = lax.broadcasted_iota(jnp.int32, (128, 128), 1) < 64
    xr = jnp.where(low, x0, pltpu.roll(x1, 64, 1))
    xi = jnp.where(low, pltpu.roll(x0, 64, 1), x1)
    zr, zi = transform(xr, xi)
    for y in range(2):
        for f in range(2):
            for c2 in range(2):
                at = slice(64 * f + 32 * c2, 64 * f + 32 * c2 + 32)
                out[pl.ds(16 * y + 4 * f + c2, 32, stride=32), :] = zr[at]
                out[pl.ds(16 * y + 4 * f + 2 + c2, 32, stride=32), :] = zi[at]

    g = got[16:17, :] + got[33:34, :]
    gr, gi = g[:, 0:1], g[:, 64:65]

    def total(k):
        return jnp.concatenate(
            [
                got[pl.ds(2 * k + c2, 32, stride=34), :] + got[pl.ds(17 + 2 * k + c2, 32, stride=34), :]
                for c2 in range(2)
            ],
            axis=0,
        )

    s1r, s1i, s2r, s2i, s3r, s3i = (total(k) for k in range(6))
    er, ei, cr, ci = zr[:64], zi[:64], zr[64:], zi[64:]
    q = 0.03125 * (cr * cr + ci * ci)
    tr = s1r - q * s2r - (cr * s3i + ci * s3r) - (er * gi + ei * gr)
    ti = s1i - q * s2i + (cr * s3r - ci * s3i) + (er * gr - ei * gi)
    pr = er - 0.03125 * ti
    pi = ei + 0.03125 * tr
    zr, zi = transform(jnp.concatenate([pr, cr], axis=0), jnp.concatenate([pi, ci], axis=0))
    for y in range(2):
        for c1 in range(4):
            at = slice(32 * c1, 32 * c1 + 32)
            out[pl.ds(16 * y + 8 + c1, 32, stride=32), :] = zr[at]
            out[pl.ds(16 * y + 12 + c1, 32, stride=32), :] = zi[at]


def place(got, fields):
    for k in range(4):
        x = jnp.concatenate([got[pl.ds(2 * k + c2, 64, stride=16), :] for c2 in range(2)], axis=0).T
        for c1 in range(4):
            fields[k, :, 128 * c1 : 128 * c1 + 128] = x[32 * c1 : 32 * c1 + 32]


def half_step(part, rates, fields, a, b, gradient, a_out, b_out, a_buf, b_buf, sem):
    copies = []
    for k in range(4):
        rows = pl.ds(8 * k, 8)

        def tile(j, _, rows=rows):
            cols = pl.ds(pl.multiple_of(part * 512 + 128 * j, 128), 128)
            here = pl.ds(pl.multiple_of(128 * j, 128), 128)
            er, ei, cr, ci = (fields[m, rows, here] for m in range(4))
            d = gradient[rows, cols]
            d3 = 0.03125 * d
            q = 0.03125 * (cr * cr + ci * ci)
            wr, wi = d3 * cr - 0.215625 * ci, 0.215625 * cr + d3 * ci
            vr, vi = d3 * cr + 0.215625 * ci, 0.215625 * cr - d3 * ci
            lr = 0.9753125 - d3 * d - q
            li = -0.24375 * d
            yr = -0.03125 * (cr * er + ci * ei)
            yi = -0.03125 * (cr * ei - ci * er)
            fr, fi = -0.21875 * ei, 0.21875 * er
            for v in range(16):
                dv3, kr, ki = (rates[3 * v + m] for m in range(3))
                ar, ai = a[0, v, rows, cols], a[1, v, rows, cols]
                br, bi = b[0, v, rows, cols], b[1, v, rows, cols]
                mr = kr - q
                gr, gi = dv3 * cr, dv3 * ci
                ur, ui = wr + gr, wi + gi
                tr, ti = vr + gr, vi - gi
                a_buf[0, v, rows, here] = (mr * ar - ki * ai) + (ur * br - ui * bi) + (fr + dv3 * er)
                a_buf[1, v, rows, here] = (mr * ai + ki * ar) + (ur * bi + ui * br) + (fi + dv3 * ei)
                b_buf[0, v, rows, here] = (lr * br - li * bi) + (tr * ar - ti * ai) + yr
                b_buf[1, v, rows, here] = (lr * bi + li * br) + (tr * ai + ti * ar) + yi
            return 0

        lax.fori_loop(0, 4, tile, 0)
        cols = pl.ds(pl.multiple_of(part * 512, 128), 512)
        for n, (src, dst) in enumerate(((a_buf, a_out), (b_buf, b_out))):
            copy = pltpu.make_async_copy(src.at[:, :, rows, :], dst.at[:, :, rows, cols], sem.at[n, k])
            copy.start()
            copies.append(copy)
    return copies


def last_part(own, other, pre, table, twiddle, post, probe_out, control_out):
    zero = lax.axis_index("co") == 0
    x = []
    for k in range(4):
        parts = []
        for comp in range(2):
            pieces = []
            for h in range(2):
                for c1 in range(4):
                    at = pl.ds(16 * k + 8 + 4 * comp + c1, 16, stride=64)
                    mine, theirs = own[at, :], other[at, :]
                    pieces.append(jnp.where(zero, *((mine, theirs) if h == 0 else (theirs, mine))))
            z = jnp.concatenate(pieces, axis=0).T
            z = [jnp.concatenate([z[64 * f : 64 * f + 32], z[64 * f + 32 : 64 * f + 64]], axis=1) for f in range(2)]
            parts.append(jnp.concatenate(z, axis=0))
        x.extend(cmul(*parts, pre[k : k + 1, :], pre[4 + k : 5 + k, :]))
    o = mm3(split(jnp.concatenate(x, axis=0)), (table[0], table[1]), ((1,), (0,)))
    r, i = [], []
    for k in range(4):
        top, low = o[128 * k : 128 * k + 64], o[128 * k + 64 : 128 * k + 128]
        yr = top[:, :256] - low[:, 256:]
        yi = top[:, 256:] + low[:, :256]
        if k:
            yr, yi = cmul(yr, yi, twiddle[k : k + 1, :], twiddle[4 + k : 5 + k, :])
        r.append(yr)
        i.append(yi)
    r, i = butterfly(r, i)
    for k in range(4):
        at = slice(256 * k, 256 * k + 256)
        yr, yi = cmul(r[k], i[k], post[0:1, at], post[1:2, at])
        probe_out[0, :, at], probe_out[1, :, at] = yr[:32], yi[:32]
        control_out[0, :, at], control_out[1, :, at] = yr[32:], yi[32:]


def near_kernel(rates, got, a, b, gradient, a_out, b_out, fields, a_buf, b_buf, sem):
    place(got, fields)
    part = lax.axis_index("co")
    for copy in half_step(part, rates, fields, a, b, gradient, a_out, b_out, a_buf, b_buf, sem):
        copy.wait()


def far_kernel(
    rates, own, other, a, b, gradient, pre, table, twiddle, post, a_in, b_in,
    a_out, b_out, probe_out, control_out, fields, a_buf, b_buf, sem, probe_buf, control_buf, last_sem,
):
    del a_in, b_in
    place(other, fields)
    part = 1 - lax.axis_index("co")
    copies = half_step(part, rates, fields, a, b, gradient, a_out, b_out, a_buf, b_buf, sem)
    last_part(own, other, pre, table, twiddle, post, probe_buf, control_buf)
    for k, (src, dst) in enumerate(((probe_buf, probe_out), (control_buf, control_out))):
        copies.append(pltpu.make_async_copy(src, dst, last_sem.at[k]))
        copies[-1].start()
    for copy in copies:
        copy.wait()


VMEM = pl.BlockSpec(memory_space=pltpu.VMEM)


ANY = pl.BlockSpec(memory_space=pl.ANY)


def f32(*shape):
    return jax.ShapeDtypeStruct(shape, F32)


def near(*shape):
    return pltpu.VMEM(shape, F32)


def pinned(arrays):
    return [pltpu.with_memory_space_constraint(jnp.asarray(x), pltpu.VMEM) for x in arrays]


def far(arrays):
    return [pltpu.with_memory_space_constraint(jnp.asarray(x), pltpu.HBM) for x in arrays]


def limit(mib):
    return pltpu.CompilerParams(vmem_limit_bytes=mib << 20)


def shards(probe, control, optical, spin, doppler, weight, gradient):
    swap = [(0, 1), (1, 0)]
    tables = [jnp.asarray(t) for t in row_tables()]
    dma = pltpu.SemaphoreType.DMA
    state = optical.shape
    own, other, fields, optical, spin, gradient, rates = pl.pallas_call(
        front_kernel,
        out_shape=(near(200, 512), near(200, 512), near(256, 128), near(*state), near(*state), near(32, N), near(48, 8, 128)),
        in_specs=[ANY] * 11,
        out_specs=(VMEM,) * 7,
        scratch_shapes=[
            pltpu.VMEM((2, 32, N), F32),
            *(pltpu.VMEM(t.shape, t.dtype) for t in tables),
            pltpu.SMEM((16,), F32),
            pltpu.SMEM((16,), F32),
            dma((2, 8)),
            dma((8,)),
        ],
        compiler_params=limit(6),
        name="front",
    )(*far([doppler, weight, optical, spin, probe, control, gradient, *tables]))
    other = lax.ppermute(other, "co", swap)
    message = pl.pallas_call(
        pack_kernel,
        out_shape=near(17 * 64, 128),
        in_specs=[VMEM] * 3,
        out_specs=VMEM,
        compiler_params=limit(6),
        name="pack",
    )(*pinned([own, other, fields]))

    def exchange(x):
        shape = x.shape
        x = lax.all_to_all(x.reshape(64, -1, 1, 128), ("space", "yh"), 0, 0, tiled=True)
        return x.reshape(shape)

    tables = column_tables()
    message = pl.pallas_call(
        columns_kernel,
        out_shape=near(N, 128),
        in_specs=[VMEM] * (1 + len(tables)),
        out_specs=VMEM,
        compiler_params=limit(6),
        name="columns",
    )(*pinned([exchange(message), *tables]))
    got = exchange(message)
    other = lax.ppermute(got, "co", swap)
    scratch = [
        pltpu.VMEM((4, 32, 512), F32),
        pltpu.VMEM((2, 16, 32, 512), F32),
        pltpu.VMEM((2, 16, 32, 512), F32),
        dma((2, 4)),
    ]
    halfway = pl.pallas_call(
        near_kernel,
        out_shape=(f32(*state), f32(*state)),
        in_specs=[VMEM] * 5,
        out_specs=(ANY, ANY),
        scratch_shapes=scratch,
        compiler_params=limit(8),
        name="near",
    )(*pinned([rates, got, optical, spin, gradient]))
    tables = last_tables()
    optical, spin, probe, control = pl.pallas_call(
        far_kernel,
        out_shape=(f32(*state), f32(*state), f32(2, 32, N), f32(2, 32, N)),
        in_specs=[VMEM] * (6 + len(tables)) + [ANY] * 2,
        out_specs=(ANY,) * 4,
        scratch_shapes=scratch + [pltpu.VMEM((2, 32, N), F32), pltpu.VMEM((2, 32, N), F32), dma((2,))],
        input_output_aliases={10: 0, 11: 1},
        compiler_params=limit(12),
        name="far",
    )(*pinned([rates, got, other, optical, spin, gradient, *tables]), *halfway)
    return probe, control, optical, spin


def solution(mesh):
    fine = Mesh(mesh.devices.reshape(mesh.devices.shape[0], 2, 2), ("space", "yh", "co"))
    vel = ("yh", "co")
    field, state = P(None, "space", None), P(None, vel, "space", None)
    return jax.shard_map(
        shards,
        mesh=fine,
        in_specs=(field, field, state, state, P(vel), P(vel), P("space", None)),
        out_specs=(field, field, state, state),
        check_vma=False,
    )
```
